32 devices in a mesh: fx: 4 (over z), fy: 4 (over x, core), fz: 2 (over y).
Axes of the slice: x: 2, y: 2, z: 4, core: 2. Of those that a mesh axis runs over, the one named last changes fastest.
Arguments:
- pressure: float32 [128, 512, 256], P('fx', 'fy', 'fz'), may hold values from -6 to 6
- source: float32 [128, 512, 256], P('fx', 'fy', 'fz'), may hold values from -6 to 6
- diag_shift: float32 [128, 512, 256], P('fx', 'fy', 'fz'), may hold values from 0.1 to 2
- iface_cells: int32 [262144], P(('fx', 'fy', 'fz')), may hold values from 0 to 524287
- iface_coef: float32 [262144], P(('fx', 'fy', 'fz')), may hold values from -6 to 6
- iface_xyz: float32 [3, 262144], P(None, ('fx', 'fy', 'fz')), may hold values from -6 to 6
- node_xyz: float32 [3, 65536], P(None, ('fx', 'fy', 'fz')), may hold values from -6 to 6
- owners: int32 [2048], P(('fx', 'fy', 'fz')), may hold values from 0 to 31, as said below
- node_lists: int32 [65536, 8], P(('fx', 'fy', 'fz')), may hold values from 0 to 1048575
Outputs:
- new_pressure: float32 [128, 512, 256], P('fx', 'fy', 'fz')
- node_loads: float32 [65536], P(('fx', 'fy', 'fz'))
The draws below stay inside these ranges and needn't reach their ends.
Inputs may be any that keep to these rules, and one draw needn't show every extreme that they name: `owners`: among the 64 tiles of one device, at most 4 have the same owner; one device owns exactly 4 tiles of every device's block; every device owns at least one tile.
All inputs are finite; a program needn't handle non-finite values.
Results may differ from the reference program's by a relative error of at most 0.0003.
Values sent between devices are 32-bit elements; how exact they have to be, the bound alone decides.
A program may use at most 192 MiB of HBM per device.

```python
import math
import jax
import jax.numpy as jnp
from jax import lax

CX = 32
CY = 128
CZ = 128
ITERS = 4
TILE = 128
CAP = 4
NODE_DEV = 2048
NEIGH = 8
OWNERS = 32
TILES_DEV = 64
NX = 128
NY = 512
NZ = 256
NTILES = 2048
NPTS = 262144
NODES = 65536
N_FY = 4
N_FZ = 2


def draw_owners(key, part):
    key_heavy, key_jitter, key_order = jax.random.split(jax.random.fold_in(key, 7031), 3)
    heavy = jax.random.randint(key_heavy, (), 0, OWNERS)
    jitter = jax.random.randint(key_jitter, (OWNERS,), 0, CAP)
    cycle_len = (OWNERS - 1) * CAP
    window = TILES_DEV - CAP
    senders = jnp.arange(OWNERS, dtype=jnp.int32)
    starts = senders * window + jitter
    spots = (starts[:, None] + jnp.arange(window, dtype=jnp.int32)[None, :]) % cycle_len
    others = (heavy + 1 + spots // CAP) % OWNERS
    heavy_part = jnp.zeros((OWNERS, CAP), jnp.int32) + heavy
    table = jnp.concatenate([heavy_part, others.astype(jnp.int32)], axis=1)
    scores = jax.random.randint(key_order, (OWNERS, TILES_DEV), 0, 1048576) * TILES_DEV
    scores = scores + jnp.arange(TILES_DEV, dtype=jnp.int32)[None, :]
    shuffle = jnp.argsort(scores, axis=1, stable=True)
    table = jnp.take_along_axis(table, shuffle, axis=1)
    return table.reshape(-1).astype(jnp.int32)


def set_ends(drawn, own_key, smallest, high):
    longest = drawn.shape.index(max(drawn.shape))
    spots = []
    for shift in (0, 1):
        where = [jax.random.randint(jax.random.fold_in(own_key, axis), (), 0, length) for axis, length in enumerate(drawn.shape)]
        where[longest] = (where[longest] + shift) % drawn.shape[longest]
        spots.append(tuple(where))
    return drawn.at[spots[0]].set(smallest).at[spots[1]].set(high)


def block_levels(own_key, dims, cuts, least, largest):
    level, own = 1.0, jax.random.fold_in(own_key, 6)
    for axis_at, shards_of in cuts:
        heights = jnp.exp(jax.random.uniform(jax.random.fold_in(own, axis_at), (shards_of,), jnp.float32, least / len(cuts), largest / len(cuts)))
        level = level * jnp.repeat(heights, dims[axis_at] // shards_of).reshape([-1 if axis == axis_at else 1 for axis in range(len(dims))])
    return level


def noise(rng, dims, spread, most, cuts=(), kind=jnp.bfloat16):
    array = jax.random.normal(rng, dims, jnp.float32) * spread
    if len(cuts) > 0:
        array = block_levels(rng, dims, cuts, -0.22, 0.18) * array
    return jnp.clip(array, min=-most, max=most).astype(kind)


def setup_inputs(seed: int = 0) -> dict:
    key_of = jax.random.split(jax.random.key(seed), 10)
    pressure = noise(key_of[0], (NX, NY, NZ), 1.0, 6.0, ((0, 4), (1, 4), (2, 2)), jnp.float32)
    source = noise(key_of[1], (NX, NY, NZ), 1.0, 6.0, ((0, 4), (1, 4), (2, 2)), jnp.float32)
    diag_shift = jnp.clip(jnp.exp(math.log(2.0) - 2.9957323 * jax.random.uniform(key_of[2], (NX, NY, NZ), jnp.float32) ** block_levels(key_of[2], (NX, NY, NZ), ((0, 4), (1, 4), (2, 2)), -0.2, 0.2)), 0.1, 2.0)
    iface_cells = set_ends(jax.random.randint(key_of[3], (NPTS,), 0, CX * CY * CZ), jax.random.fold_in(key_of[3], 1), 0, (CX * CY * CZ) - 1).astype(jnp.int32)
    iface_coef = noise(key_of[4], (NPTS,), 1.0, 6.0, ((0, 32),), jnp.float32)
    iface_xyz = noise(key_of[5], (3, NPTS), 1.0, 6.0, ((1, 32),), jnp.float32)
    node_xyz = noise(key_of[6], (3, NODES), 1.0, 6.0, ((1, 32),), jnp.float32)
    owners = draw_owners(jax.random.fold_in(key_of[9], 71), 0)
    node_lists = set_ends(jax.random.randint(key_of[8], (NODES, NEIGH), 0, 1048576), jax.random.fold_in(key_of[8], 1), 0, 1048575).astype(jnp.int32)
    return dict(pressure=pressure, source=source, diag_shift=diag_shift, iface_cells=iface_cells, iface_coef=iface_coef, iface_xyz=iface_xyz, node_xyz=node_xyz, owners=owners, node_lists=node_lists)


GAUSS_RATE = 0.5


def jacobi_step(pressure_now, source, diag_shift):
    neighbours = jnp.roll(pressure_now, 1, 0) + jnp.roll(pressure_now, -1, 0)
    neighbours = neighbours + jnp.roll(pressure_now, 1, 1) + jnp.roll(pressure_now, -1, 1)
    neighbours = neighbours + jnp.roll(pressure_now, 1, 2) + jnp.roll(pressure_now, -1, 2)
    return (neighbours + source) / (6.0 + diag_shift)


def reference(pressure, source, diag_shift, iface_cells, iface_coef, iface_xyz, node_xyz, owners, node_lists):
    points = jnp.arange(NPTS, dtype=jnp.int32)
    holder = points // (TILES_DEV * TILE)
    block_x = holder // (N_FY * N_FZ)
    block_y = (holder // N_FZ) % N_FY
    block_z = holder % N_FZ
    cell_x = block_x * CX + iface_cells // (CY * CZ)
    cell_y = block_y * CY + (iface_cells // CZ) % CY
    cell_z = block_z * CZ + iface_cells % CZ
    values = iface_coef * pressure[cell_x, cell_y, cell_z]
    pressure_now = pressure
    for sweep_index in range(ITERS):
        pressure_now = jacobi_step(pressure_now, source, diag_shift)
    counts = jnp.bincount(owners, length=OWNERS).astype(jnp.int32)
    grouped = jnp.argsort(owners, stable=True).astype(jnp.int32)
    offsets = (jnp.cumsum(counts) - counts).astype(jnp.int32)
    tile_values = values.reshape(NTILES, TILE)
    tile_xyz = iface_xyz.reshape(3, NTILES, TILE)

    def one_owner(inputs):
        owner_id, coords, entries = inputs
        chosen = grouped[offsets[owner_id] + entries % counts[owner_id]]
        distance = jnp.zeros((NODE_DEV, NEIGH, TILE), jnp.float32)
        for component in range(3):
            gap_axis = coords[component][:, None, None] - tile_xyz[component][chosen]
            distance = distance + gap_axis * gap_axis
        return jnp.sum(jnp.exp(-GAUSS_RATE * distance) * tile_values[chosen], axis=(1, 2))

    owner_ids = jnp.arange(OWNERS, dtype=jnp.int32)
    node_coords = node_xyz.reshape(3, OWNERS, NODE_DEV).transpose(1, 0, 2)
    node_entries = node_lists.reshape(OWNERS, NODE_DEV, NEIGH)
    node_loads = lax.map(one_owner, (owner_ids, node_coords, node_entries))
    return pressure_now, node_loads.reshape(NODES)
```

```python
import functools
import math

import jax
import jax.numpy as jnp
from jax import lax
from jax.experimental import pallas as pl
from jax.experimental.pallas import tpu as pltpu
from jax.sharding import PartitionSpec as P

ITERS = 4
CAP = 4
GAUSS_RATE = 0.5
SCALE = math.sqrt(GAUSS_RATE * math.log2(math.e))
FAR = 1.0e6
NODE_BLOCK = 256
MESH = pl.DeviceIdType.MESH
F32 = jnp.float32
BF16 = jnp.bfloat16


def split2(x):
    hi = x.astype(BF16)
    return hi, (x - hi.astype(F32)).astype(BF16)


def split3(x):
    hi = x.astype(BF16)
    rest = x - hi.astype(F32)
    mid = rest.astype(BF16)
    return hi, mid, (rest - mid.astype(F32)).astype(BF16)


def mm(a, b):
    return jnp.dot(a, b, preferred_element_type=F32)


def iota(shape, dim):
    return lax.broadcasted_iota(jnp.int32, shape, dim)


def ones_where(mask):
    return jnp.where(mask, 1.0, 0.0).astype(BF16)


def route_kernel(
    devices, cells_s, table, cells, coef, xyz, owners, out, rows, parts
):
    tiles, width = cells.shape
    lanes = table.shape[1]
    shift = lanes.bit_length() - 1

    def fetch(t, carry):
        base = t * width
        for p in range(width):
            at = lax.shift_right_logical(cells_s[base + p], shift)
            rows[pl.ds(base + p, 1), :] = table[pl.ds(at, 1), :]
        return carry

    lax.fori_loop(0, tiles, fetch, 0)

    diagonal = iota((width, width), 0) == iota((width, width), 1)

    def pick(t, carry):
        base = pl.multiple_of(t * width, width)
        hi, lo = split2(rows[pl.ds(base, width), :])
        lane = jnp.bitwise_and(cells[pl.ds(t, 1), :], lanes - 1)
        chosen = ones_where(iota((lanes, width), 0) == lane)
        got = mm(hi, chosen) + mm(lo, chosen)
        got = jnp.sum(jnp.where(diagonal, got, 0.0), axis=0, keepdims=True)
        parts[3, pl.ds(t, 1), :] = got * coef[pl.ds(t, 1), :]
        for c in range(3):
            parts[c, pl.ds(t, 1), :] = xyz[c : c + 1, pl.ds(base, width)]
        return carry

    lax.fori_loop(0, tiles, pick, 0, unroll=2)

    own = owners[...]
    mine = iota((devices, tiles), 0) == own
    before = ones_where(iota((tiles, tiles), 0) < iota((tiles, tiles), 1))
    earlier = mm(ones_where(mine), before)
    rank = jnp.sum(jnp.where(mine, earlier, 0.0), axis=0, keepdims=True)
    target = own * CAP + rank.astype(jnp.int32)
    line = iota((devices * 8, tiles), 0)
    at_slot = (line // 8) * CAP + line % CAP == target
    low = line % 8 < CAP
    first = ones_where(at_slot & low)
    second = ones_where(at_slot & jnp.logical_not(low))
    filled = mm(first, jnp.ones((tiles, width), BF16))
    for half in range(2):
        total = None
        for sel, c in ((first, 2 * half), (second, 2 * half + 1)):
            for piece in split3(parts[c]):
                term = mm(sel, piece)
                total = term if total is None else total + term
        if half == 0:
            empty = (iota(filled.shape, 0) % 8 < CAP) & (filled < 0.5)
            total = jnp.where(empty, FAR, total)
        out[half] = total.reshape(devices, 8, width)


def main_kernel(
    sizes,
    p_any, s_any, d_any, outgoing, nodes, lists,
    new_p, loads,
    a_buf, b_buf, src, inv, hx, hy, hz, ys, zs, incoming, tab, pos, want,
    load_sem, x_send, x_recv, y_send, y_recv, z_send, z_recv, t_send, t_recv,
):
    nfx, nfy, nfz = sizes
    devices = nfx * nfy * nfz
    cx, cy, cz = src.shape
    width = outgoing.shape[-1]
    bx, by, bz = lax.axis_index("fx"), lax.axis_index("fy"), lax.axis_index("fz")
    me = (bx * nfy + by) * nfz + bz
    pad = 8
    body = pl.ds(pad, cy)

    load_p = pltpu.make_async_copy(p_any, a_buf.at[:, body, :], load_sem.at[0])
    load_s = pltpu.make_async_copy(s_any, src, load_sem.at[1])
    load_d = pltpu.make_async_copy(d_any, inv, load_sem.at[2])
    load_p.start()
    load_s.start()
    load_d.start()

    def coords(flat):
        return (flat // (nfy * nfz), (flat // nfz) % nfy, flat % nfz)

    barrier = pltpu.get_barrier_semaphore()

    def greet(o, carry):
        pl.semaphore_signal(
            barrier, inc=1, device_id=coords((me + o) % devices), device_id_type=MESH
        )
        return carry

    lax.fori_loop(1, devices, greet, 0)
    pl.semaphore_wait(barrier, devices - 1)

    def remote(a, b, ss, rs, device):
        return pltpu.make_async_remote_copy(
            src_ref=a, dst_ref=b, send_sem=ss, recv_sem=rs, device_id=device, device_id_type=MESH
        )

    def tile_copy(o):
        to = (me + o) % devices
        return remote(
            outgoing.at[:, to], incoming.at[:, me], t_send.at[o], t_recv.at[o], coords(to)
        )

    x_next, x_prev = ((bx + 1) % nfx, by, bz), ((bx + nfx - 1) % nfx, by, bz)
    y_next, y_prev = (bx, (by + 1) % nfy, bz), (bx, (by + nfy - 1) % nfy, bz)
    z_next, z_prev = (bx, by, (bz + 1) % nfz), (bx, by, (bz + nfz - 1) % nfz)

    def x_copies(it, buf):
        return [
            remote(buf.at[cx - 1, body], hx.at[it, 0], x_send.at[it, 0], x_recv.at[it, 0], x_next),
            remote(buf.at[0, body], hx.at[it, 1], x_send.at[it, 1], x_recv.at[it, 1], x_prev),
        ]

    def yz_copies(it):
        made = [
            remote(ys.at[it, 1], hy.at[it, 0], y_send.at[it, 0], y_recv.at[it, 0], y_next),
            remote(ys.at[it, 0], hy.at[it, 1], y_send.at[it, 1], y_recv.at[it, 1], y_prev),
            remote(zs.at[it], hz.at[it, 0], z_send.at[it, 0], z_recv.at[it, 0], z_next),
        ]
        if nfz > 2:
            made.append(
                remote(zs.at[it], hz.at[it, 1], z_send.at[it, 1], z_recv.at[it, 1], z_prev)
            )
        return made

    lane = iota((cy, cz), 1)
    pair = lax.shift_right_logical(lane, 1)

    def faces(it, x, plane, packed):
        ys[it, 0, pl.ds(x, 1), :] = plane[0:1]
        ys[it, 1, pl.ds(x, 1), :] = plane[cy - 1 : cy]
        return jnp.where(pair == x, pltpu.roll(plane, 2 * x + 1, 1), packed)

    load_p.wait()
    started = [x_copies(0, a_buf)]
    for c in started[0]:
        c.start()

    def first_faces(x, packed):
        return faces(0, x, a_buf[x, pl.ds(pad, cy), :], packed)

    zs[0] = lax.fori_loop(0, cx, first_faces, jnp.zeros((cy, cz), F32))
    started[0] = started[0] + yz_copies(0)
    for c in started[0][2:]:
        c.start()

    def send_tile(o, carry):
        tile_copy(o).start()
        return carry

    lax.fori_loop(1, devices, send_tile, 0)
    incoming[:, me] = outgoing[:, me]
    load_s.wait()
    load_d.wait()

    def sweep(it, cur, nxt):
        last = it == ITERS - 1
        for c in started[it]:
            c.wait_recv()
        if it > 0:
            for c in started[it - 1][:2]:
                c.wait_send()

        def rows(x, carry):
            cur[x, pl.ds(pad - 1, 1), :] = hy[it, 0, pl.ds(x, 1), :]
            cur[x, pl.ds(pad + cy, 1), :] = hy[it, 1, pl.ds(x, 1), :]
            return carry

        lax.fori_loop(0, cx, rows, 0, unroll=4)
        if nfz > 2:
            hz[it, 0] = jnp.where(lane % 2 == 0, hz[it, 0], hz[it, 1])

        def plane(x, below, above, packed):
            mid = cur[x, pl.ds(pad, cy), :]
            edge = pltpu.roll(hz[it, 0], cz - 1 - 2 * x, 1)
            total = pltpu.roll(jnp.where(lane == 0, edge, mid), cz - 1, 1)
            total = total + pltpu.roll(jnp.where(lane == cz - 1, edge, mid), 1, 1)
            total = total + cur[x, pl.ds(pad - 1, cy), :]
            total = total + cur[x, pl.ds(pad + 1, cy), :]
            total = total + below + above + src[x]
            if it == 0:
                scale = 1.0 / (6.0 + inv[x])
                inv[x] = scale
            else:
                scale = inv[x]
            new = total * scale
            if last:
                new_p[x] = new
                return packed
            nxt[x, pl.ds(pad, cy), :] = new
            return faces(it + 1, x, new, packed)

        def at(x):
            return cur[x, pl.ds(pad, cy), :]

        packed = jnp.zeros((cy, cz), F32) if not last else jnp.int32(0)
        packed = plane(0, hx[it, 0], at(1), packed)
        packed = plane(cx - 1, at(cx - 2), hx[it, 1], packed)
        if not last:
            started.append(x_copies(it + 1, nxt))
            for c in started[-1]:
                c.start()
        packed = lax.fori_loop(
            1, cx - 1, lambda x, z: plane(x, at(x - 1), at(x + 1), z), packed
        )
        if not last:
            zs[it + 1] = packed
            more = yz_copies(it + 1)
            for c in more:
                c.start()
            started[-1] = started[-1] + more

    slots = devices * CAP
    lines = devices * 8

    def prepare():
        def wait_tile(o, carry):
            tile_copy(o).wait_recv()
            return carry

        lax.fori_loop(1, devices, wait_tile, 0)
        low = incoming[0].reshape(lines, width)
        high = incoming[1].reshape(lines, width)
        row = iota((lines, slots), 0)
        col = iota((lines, slots), 1)
        home = (row // 8) * CAP + row % CAP
        lower = row % 8 < CAP
        take = (ones_where((home == col) & lower), ones_where((home == col) & (row % 8 >= CAP)))
        for half, block in ((0, low), (1, high)):
            turned = block.T
            for second in range(2):
                c = 2 * half + second
                scaled = turned if c == 3 else turned * SCALE
                hi, lo = split2(scaled)
                tab[c * width : (c + 1) * width, 0:slots] = mm(hi, take[second]).astype(BF16)
                tab[c * width : (c + 1) * width, slots : 2 * slots] = mm(lo, take[second]).astype(
                    BF16
                )
        here = ones_where(low < 0.5 * FAR)
        row = iota((slots, lines), 0)
        col = iota((slots, lines), 1)
        home = (col // 8) * CAP + col % CAP
        lower = col % 8 < CAP
        prefix = mm(ones_where((home <= row) & lower), here)
        there = mm(ones_where((home == row) & lower), here)
        place = jnp.where(there > 0.5, prefix - 1.0, -1.0)
        pos[:, 0:width] = place
        pos[:, width : 2 * width] = place
        count = prefix[slots - 1 : slots, 0:1]
        entry = lists[...].astype(F32)
        rest = entry - jnp.floor(entry / count) * count
        rest = jnp.where(rest < 0.0, rest + count, rest)
        want[...] = jnp.where(rest >= count, rest - count, rest)

    neigh = lists.shape[0]

    def gauss(block, carry):
        span = pl.ds(pl.multiple_of(block * NODE_BLOCK, NODE_BLOCK), NODE_BLOCK)
        here = [nodes[c : c + 1, span] * SCALE for c in range(3)]
        total = jnp.zeros((8, NODE_BLOCK), F32)
        for k in range(neigh):
            hot = ones_where(pos[...] == want[k : k + 1, span])
            hot = jnp.concatenate([hot, hot], axis=0)
            got = mm(tab[...], hot)
            far = None
            for c in range(3):
                gap = got[c * width : (c + 1) * width] - here[c]
                far = gap * gap if far is None else far + gap * gap
            term = jnp.exp2(-far) * got[3 * width : 4 * width]
            total = total + jnp.sum(term.reshape(width // 8, 8, NODE_BLOCK), axis=0)
        loads[:, span] = jnp.sum(total, axis=0, keepdims=True)
        return carry

    blocks = nodes.shape[1] // NODE_BLOCK
    bounds = [blocks * i // (ITERS - 1) for i in range(ITERS)]
    bufs = (a_buf, b_buf)
    for it in range(ITERS):
        sweep(it, bufs[it % 2], bufs[(it + 1) % 2])
        if it == 0:
            prepare()
        if it < ITERS - 1:
            lax.fori_loop(bounds[it], bounds[it + 1], gauss, 0)

    for it, group in enumerate(started):
        for c in group if it == ITERS - 1 else group[2:]:
            c.wait_send()

    def drain(o, carry):
        tile_copy(o).wait_send()
        return carry

    lax.fori_loop(1, devices, drain, 0)


def on_device(
    sizes,
    pressure, source, diag_shift, iface_cells, iface_coef, iface_xyz, node_xyz, owners, node_lists,
):
    nfx, nfy, nfz = sizes
    devices = nfx * nfy * nfz
    tiles = owners.shape[0]
    width = iface_coef.shape[0] // tiles
    cx, cy, cz = pressure.shape
    nodes, neigh = node_lists.shape
    vmem = pl.BlockSpec(memory_space=pltpu.VMEM)
    smem = pl.BlockSpec(memory_space=pltpu.SMEM)
    hbm = pl.BlockSpec(memory_space=pl.ANY)
    slots = devices * CAP
    outgoing = pl.pallas_call(
        functools.partial(route_kernel, devices),
        out_shape=jax.ShapeDtypeStruct((2, devices, 8, width), F32),
        in_specs=[smem] + [vmem] * 5,
        out_specs=vmem,
        scratch_shapes=[
            pltpu.VMEM((tiles * width, cz), F32),
            pltpu.VMEM((4, tiles, width), F32),
        ],
        compiler_params=pltpu.CompilerParams(vmem_limit_bytes=48 * 1024 * 1024),
        name="route",
    )(
        iface_cells,
        pressure.reshape(cx * cy, cz),
        iface_cells.reshape(tiles, width),
        iface_coef.reshape(tiles, width),
        iface_xyz,
        owners.reshape(1, tiles),
    )
    dma = pltpu.SemaphoreType.DMA
    new_p, loads = pl.pallas_call(
        functools.partial(main_kernel, sizes),
        out_shape=(
            jax.ShapeDtypeStruct((cx, cy, cz), F32),
            jax.ShapeDtypeStruct((1, nodes), F32),
        ),
        in_specs=[hbm] * 3 + [vmem] * 3,
        out_specs=(vmem, vmem),
        scratch_shapes=[
            pltpu.VMEM((cx, cy + 16, cz), F32),
            pltpu.VMEM((cx, cy + 16, cz), F32),
            pltpu.VMEM((cx, cy, cz), F32),
            pltpu.VMEM((cx, cy, cz), F32),
            pltpu.VMEM((ITERS, 2, cy, cz), F32),
            pltpu.VMEM((ITERS, 2, cx, cz), F32),
            pltpu.VMEM((ITERS, 2, cy, cz), F32),
            pltpu.VMEM((ITERS, 2, cx, cz), F32),
            pltpu.VMEM((ITERS, cy, cz), F32),
            pltpu.VMEM((2, devices, 8, width), F32),
            pltpu.VMEM((4 * width, 2 * slots), BF16),
            pltpu.VMEM((slots, NODE_BLOCK), F32),
            pltpu.VMEM((neigh, nodes), F32),
            dma((3,)),
            dma((ITERS, 2)), dma((ITERS, 2)),
            dma((ITERS, 2)), dma((ITERS, 2)),
            dma((ITERS, 2)), dma((ITERS, 2)),
            dma((devices,)), dma((devices,)),
        ],
        compiler_params=pltpu.CompilerParams(
            collective_id=0, has_side_effects=True, vmem_limit_bytes=56 * 1024 * 1024
        ),
        name="sweeps",
    )(pressure, source, diag_shift, outgoing, node_xyz, node_lists.T)
    return new_p, loads.reshape(nodes)


def solution(mesh):
    sizes = tuple(mesh.shape[a] for a in ("fx", "fy", "fz"))
    cells = P("fx", "fy", "fz")
    flat = P(("fx", "fy", "fz"))
    return jax.shard_map(
        functools.partial(on_device, sizes),
        mesh=mesh,
        in_specs=(
            cells, cells, cells, flat, flat,
            P(None, ("fx", "fy", "fz")), P(None, ("fx", "fy", "fz")), flat,
            P(("fx", "fy", "fz"), None),
        ),
        out_specs=(cells, flat),
        check_vma=False,
    )
```
